128 devices in a mesh: row: 16 (over y_lo, z, core), col: 8 (over x, y_hi).
Axes of the slice: x: 4, y: 4 (y_hi: 2, y_lo: 2; y = y_hi * 2 + y_lo), z: 4, core: 2. Of those that a mesh axis runs over, the one named last changes fastest.
Arguments:
- coarse_kernel: bfloat16 [2048, 128, 128], P(('row', 'col')), may hold values from -6 to 6
- interp_index: int32 [16384, 4], P(('row', 'col')), may hold values from 0 to 2047, as said below
- interp_weight: float32 [16384, 4], P(('row', 'col')), may hold values from 0.2 to 1
- left_rot: bfloat16 [16384, 128, 128], P(('row', 'col')), may hold values from -0.5 to 0.5
- right_rot: bfloat16 [16384, 128, 128], P(('row', 'col')), may hold values from -0.5 to 0.5
- trial: bfloat16 [16384, 2048], P('col'), may hold values from -0.046875 to 0.046875
Outputs:
- product: float32 [16384, 2048], P('row', 'col')
The draws below stay inside these ranges and needn't reach their ends.
Inputs may be any that keep to these rules, and one draw needn't show every extreme that they name: `interp_index`: within each aligned run of 128 fine blocks (the rows of one device), the entries name at most 2 different coarse blocks from any aligned group of 16 coarse blocks, and exactly 2 from at least one group.
All inputs are finite; a program needn't handle non-finite values.
Results may differ from the reference program's by a relative error of at most 0.0029.
Values may be sent and summed in bfloat16 or wider, within the bound.
No kernel may reach another device: no remote copies, remote signals or barrier semaphores. Data moves between devices by JAX's collectives and lax.ppermute only.
A program may use at most 128 MiB of HBM per device.

```python
import jax
import jax.numpy as jnp
from jax import lax

BS = 128
TR = 8
TC = 16
NV = 2048
CB_DEV = 16
CAP = 2
BLK_DEV = 128
FINE = 16384
NB = 2048
PANEL_COLS = 16384
N_ROW = 16
N_COL = 8


def draw_interp_index(key, part):
    dev_count = NB // CB_DEV
    total = dev_count * CAP

    def one_device(device):
        base = jax.random.fold_in(jax.random.fold_in(key, 7), device)
        key_count, key_perm, key_fill, key_order = jax.random.split(base, 4)
        counts = jax.random.randint(key_count, (dev_count,), 0, CAP + 1)
        forced = (device * 5 + 3) % dev_count
        counts = jnp.where(jnp.arange(dev_count) == forced, CAP, counts)
        perm_keys = jax.random.split(key_perm, dev_count)
        local_ids = jax.vmap(lambda sub_key: jax.random.permutation(sub_key, CB_DEV)[:CAP])(perm_keys)
        candidate = (jnp.arange(dev_count)[:, None] * CB_DEV + local_ids).reshape(-1)
        valid = (jnp.arange(CAP)[None, :] < counts[:, None]).reshape(-1)
        order = jnp.argsort(jnp.where(valid, 0, 1) * total + jnp.arange(total))
        listed = candidate[order]
        live = jnp.sum(valid.astype(jnp.int32))
        position = jnp.arange(4 * BLK_DEV)
        extra = jax.random.randint(key_fill, (4 * BLK_DEV,), 0, live)
        chosen = listed[jnp.where(position < live, position, extra)]
        chosen = jax.random.permutation(key_order, chosen)
        return chosen.reshape(BLK_DEV, 4)
    return jax.vmap(one_device)(jnp.arange(dev_count)).reshape(FINE, 4).astype(jnp.int32)


def block_scale(rng, shape, cuts, low, top_value):
    factor_of = 1.0
    for dim, shards_of in cuts:
        steps = jax.random.uniform(jax.random.fold_in(jax.random.fold_in(rng, 6), dim), (shards_of,), jnp.float32, low / len(cuts), top_value / len(cuts))
        factor_of = factor_of * jnp.repeat(jnp.exp(steps), shape[dim] // shards_of).reshape((-1,) + (1,) * (len(shape) - 1 - dim))
    return factor_of


def scatter_about(key, shape, width, limit, cuts=(), kind=jnp.bfloat16):
    values = width * jax.random.normal(key, shape, jnp.float32)
    if cuts:
        values = values * block_scale(key, shape, cuts, -0.22, 0.18)
    return jnp.clip(values, -limit, limit).astype(kind)


def setup_inputs(seed: int = 0) -> dict:
    arg_keys = jax.random.split(jax.random.key(seed), 7)
    return {
        "coarse_kernel": scatter_about(arg_keys[0], (NB, BS, BS), 1.0, 6.0, ((0, 128),)),
        "interp_index": draw_interp_index(jax.random.fold_in(arg_keys[6], 71), 0),
        "interp_weight": jnp.clip(0.2 + 0.8 * jax.random.uniform(arg_keys[2], (FINE, 4), jnp.float32) ** block_scale(arg_keys[2], (FINE, 4), ((0, 128),), -0.2, 0.2), 0.2, 1.0),
        "left_rot": scatter_about(arg_keys[3], (FINE, BS, BS), BS ** -0.5, 0.5, ((0, 128),)),
        "right_rot": scatter_about(arg_keys[4], (FINE, BS, BS), BS ** -0.5, 0.5, ((0, 128),)),
        "trial": scatter_about(arg_keys[5], (PANEL_COLS, NV), PANEL_COLS ** -0.5, 0.046875, ((0, 8),)),
    }


def fine_set(coarse_kernel, pieces):
    index_rows, weight_rows, left_rows, right_rows = pieces
    picked = jnp.take(coarse_kernel, index_rows.reshape(-1), axis=0).reshape(index_rows.shape[0], 4, BS, BS)
    merged = jnp.sum(weight_rows[:, :, None, None] * picked.astype(jnp.float32), axis=1)
    turned = jnp.einsum("fab,fbc->fac", left_rows.astype(jnp.float32), merged, precision=lax.Precision.HIGHEST)
    return jnp.einsum("fac,fdc->fad", turned, right_rows.astype(jnp.float32), precision=lax.Precision.HIGHEST).astype(jnp.bfloat16)


def reference(coarse_kernel, interp_index, interp_weight, left_rot, right_rot, trial):
    dev_count = N_ROW * N_COL
    share = BLK_DEV // dev_count
    pieces = (interp_index.reshape(dev_count, BLK_DEV, 4), interp_weight.reshape(dev_count, BLK_DEV, 4),
              left_rot.reshape(dev_count, BLK_DEV, BS, BS), right_rot.reshape(dev_count, BLK_DEV, BS, BS))
    fine_blocks = lax.map(lambda piece: fine_set(coarse_kernel, piece), pieces)
    fine_blocks = fine_blocks.reshape(dev_count, dev_count, share, BS, BS)
    fine_blocks = jnp.transpose(fine_blocks, (1, 0, 2, 3, 4)).reshape(N_ROW, N_COL, TR, TC, BS, BS)
    panel = jnp.transpose(fine_blocks, (0, 2, 4, 1, 3, 5)).reshape(N_ROW * TR * BS, N_COL * TC * BS)
    return jnp.dot(panel, trial, preferred_element_type=jnp.float32)
```

```python
import jax
import jax.numpy as jnp
from jax import lax
from jax.experimental import pallas as pl
from jax.experimental.pallas import tpu as pltpu
from jax.sharding import PartitionSpec as P

TC = 16
CAP = 2
STEP = 8


def serve_kernel(wanted, coarse, out, sem):
    count = out.shape[0]

    def issue(i, carry):
        pltpu.make_async_copy(coarse.at[wanted[i]], out.at[i], sem).start()
        return carry

    lax.fori_loop(0, count, issue, 0, unroll=8)
    pltpu.make_async_copy(out, out, sem).wait()


def serve(wanted, coarse_kernel):
    count = wanted.shape[0]
    return pl.pallas_call(
        serve_kernel,
        grid_spec=pltpu.PrefetchScalarGridSpec(
            num_scalar_prefetch=1,
            grid=(),
            in_specs=[pl.BlockSpec(memory_space=pltpu.VMEM)],
            out_specs=pl.BlockSpec(memory_space=pl.ANY),
            scratch_shapes=[pltpu.SemaphoreType.DMA],
        ),
        out_shape=jax.ShapeDtypeStruct((count,) + coarse_kernel.shape[1:], coarse_kernel.dtype),
        name="serve",
    )(wanted, coarse_kernel)


def split(value):
    high = value.astype(jnp.bfloat16)
    low = (value - high.astype(jnp.float32)).astype(jnp.bfloat16)
    return high, low


def rotate_kernel(slots, weights, arrived, left, right, out):
    base = pl.program_id(0) * left.shape[0]
    for k in range(left.shape[0]):
        f = (base + k) * 4
        merged = weights[f] * arrived[slots[f]].astype(jnp.float32)
        for j in range(1, 4):
            merged += weights[f + j] * arrived[slots[f + j]].astype(jnp.float32)
        lhs = left[k]
        turned = jnp.dot(
            jnp.concatenate([lhs, lhs], axis=1),
            jnp.concatenate(split(merged), axis=0),
            preferred_element_type=jnp.float32,
        )
        rhs = right[k]
        fine = lax.dot_general(
            jnp.concatenate(split(turned), axis=1),
            jnp.concatenate([rhs, rhs], axis=1),
            (((1,), (1,)), ((), ())),
            preferred_element_type=jnp.float32,
        )
        out[k] = fine.astype(jnp.bfloat16)


def rotate(slots, weights, arrived, left, right):
    blocks, size, _ = left.shape
    spec = pl.BlockSpec((STEP, size, size), lambda i, *_: (i, 0, 0))
    return pl.pallas_call(
        rotate_kernel,
        grid_spec=pltpu.PrefetchScalarGridSpec(
            num_scalar_prefetch=2,
            grid=(blocks // STEP,),
            in_specs=[pl.BlockSpec(memory_space=pltpu.VMEM), spec, spec],
            out_specs=spec,
        ),
        out_shape=jax.ShapeDtypeStruct(left.shape, jnp.bfloat16),
        name="rotate",
    )(slots, weights, arrived, left, right)


def panel_kernel(tile, vectors, out):
    parts, _, width = out.shape
    lhs = jnp.concatenate([tile[b] for b in range(TC)], axis=1)
    for part in range(parts):
        out[part] = jnp.dot(
            lhs, vectors[:, part * width : (part + 1) * width], preferred_element_type=jnp.float32
        ).astype(jnp.bfloat16)


def panel_product(gridded, trial, parts):
    blocks, size, _ = gridded.shape
    width = trial.shape[1] // parts
    rows = blocks // TC
    return pl.pallas_call(
        panel_kernel,
        grid=(rows,),
        in_specs=[
            pl.BlockSpec((TC, size, size), lambda a: (a, 0, 0)),
            pl.BlockSpec(memory_space=pltpu.VMEM),
        ],
        out_specs=pl.BlockSpec((parts, size, width), lambda a: (0, a, 0)),
        out_shape=jax.ShapeDtypeStruct((parts, rows * size, width), jnp.bfloat16),
        name="panel",
    )(gridded, trial)


def shards(coarse_kernel, interp_index, interp_weight, left_rot, right_rot, trial):
    col_count = lax.axis_size("col")
    dev_count = lax.axis_size("row") * col_count
    coarse_per = coarse_kernel.shape[0]
    ref_ids = interp_index.reshape(-1)
    catalog = jnp.arange(dev_count * coarse_per, dtype=jnp.int32)
    needed = (
        jnp.any(ref_ids[:, None] == catalog[None, :], axis=0)
        .astype(jnp.int32)
        .reshape(dev_count, coarse_per)
    )
    slot_rank = jnp.cumsum(needed, axis=1) - needed
    picker = needed[:, :, None] * (
        slot_rank[:, :, None] == jnp.arange(CAP, dtype=jnp.int32)[None, None, :]
    ).astype(jnp.int32)
    wanted = jnp.sum(picker * jnp.arange(coarse_per, dtype=jnp.int32)[None, :, None], axis=1)
    requested = lax.all_to_all(wanted, ("row", "col"), split_axis=0, concat_axis=0, tiled=True)
    served = serve(requested.reshape(-1), coarse_kernel).reshape(
        (dev_count, CAP) + coarse_kernel.shape[1:]
    )
    arrived = lax.all_to_all(served, ("row", "col"), split_axis=0, concat_axis=0, tiled=True)
    arrived = arrived.reshape((dev_count * CAP,) + coarse_kernel.shape[1:])
    slot_table = (jnp.arange(dev_count, dtype=jnp.int32)[:, None] * CAP + slot_rank).reshape(-1)
    ref_slots = jnp.take(slot_table, ref_ids, mode="clip")
    fine_blocks = rotate(ref_slots, interp_weight.reshape(-1), arrived, left_rot, right_rot)
    gridded = lax.all_to_all(fine_blocks, ("row", "col"), split_axis=0, concat_axis=0, tiled=True)
    partial_product = panel_product(gridded, trial, col_count)
    shares = lax.all_to_all(partial_product, "col", split_axis=0, concat_axis=0, tiled=True)
    return jnp.sum(shares.astype(jnp.float32), axis=0)


def solution(mesh):
    return jax.shard_map(
        shards,
        mesh=mesh,
        in_specs=(
            P(("row", "col"), None, None),
            P(("row", "col"), None),
            P(("row", "col"), None),
            P(("row", "col"), None, None),
            P(("row", "col"), None, None),
            P("col", None),
        ),
        out_specs=P("row", "col"),
        check_vma=False,
    )
```

```python
import functools

import jax
import jax.numpy as jnp
from jax import lax
from jax.experimental import pallas as pl
from jax.experimental.pallas import tpu as pltpu
from jax.sharding import Mesh, PartitionSpec as P

CAP = 2
UNROLL = 16
CHUNKS = 4
ALL = ("ylo", "z", "core", "x", "yhi")
COL = ("x", "yhi")
SAME_CORE = ("ylo", "z", "x", "yhi")


def serve_kernel(wanted, coarse, out, sem):
    def issue(i, carry):
        pltpu.make_async_copy(coarse.at[wanted[i]], out.at[i], sem).start()
        return carry

    lax.fori_loop(0, out.shape[0], issue, 0, unroll=8)
    pltpu.make_async_copy(out, out, sem).wait()


def serve(wanted, coarse_kernel):
    count = wanted.shape[0]
    return pl.pallas_call(
        serve_kernel,
        grid_spec=pltpu.PrefetchScalarGridSpec(
            num_scalar_prefetch=1,
            grid=(),
            in_specs=[pl.BlockSpec(memory_space=pltpu.VMEM)],
            out_specs=pl.BlockSpec(memory_space=pl.ANY),
            scratch_shapes=[pltpu.SemaphoreType.DMA],
        ),
        out_shape=jax.ShapeDtypeStruct((count,) + coarse_kernel.shape[1:], coarse_kernel.dtype),
        name="serve",
    )(wanted, coarse_kernel)


def split(value):
    high = value.astype(jnp.bfloat16)
    low = (value - high.astype(jnp.float32)).astype(jnp.bfloat16)
    return high, low


def rotate_kernel(
    core, slots, weights, arrived, left, right, mine, theirs,
    arrived_v, left_v, right_v, out_v, sem_arrived, sem_left, sem_right, sem_mine, sem_theirs,
):
    blocks = left.shape[0]
    span = blocks // CHUNKS
    groups = mine.shape[0] // 8
    copies = []
    first = pltpu.make_async_copy(arrived, arrived_v, sem_arrived)
    first.start()
    for n in range(CHUNKS):
        part = pl.ds(n * span, span)
        pair = (
            pltpu.make_async_copy(left.at[part], left_v.at[part], sem_left.at[n]),
            pltpu.make_async_copy(right.at[part], right_v.at[part], sem_right.at[n]),
        )
        for copy in pair:
            copy.start()
        copies.append(pair)
    first.wait()

    def block(f):
        r = f * 4
        merged = weights[r] * arrived_v[slots[r]].astype(jnp.float32)
        for j in range(1, 4):
            merged += weights[r + j] * arrived_v[slots[r + j]].astype(jnp.float32)
        lhs = left_v[f]
        turned = jnp.dot(
            jnp.concatenate([lhs, lhs], axis=1),
            jnp.concatenate(split(merged), axis=0),
            preferred_element_type=jnp.float32,
        )
        rhs = right_v[f]
        fine = lax.dot_general(
            jnp.concatenate(split(turned), axis=1),
            jnp.concatenate([rhs, rhs], axis=1),
            (((1,), (1,)), ((), ())),
            preferred_element_type=jnp.float32,
        )
        out_v[f] = fine.astype(jnp.bfloat16)

    for n in range(CHUNKS):
        for copy in copies[n]:
            copy.wait()

        def several(i, carry):
            for k in range(UNROLL):
                block(n * span + i * UNROLL + k)
            return carry

        lax.fori_loop(0, span // UNROLL, several, 0)
        for g in range(n * groups // CHUNKS, (n + 1) * groups // CHUNKS):
            pltpu.make_async_copy(
                out_v.at[pl.ds(g * 16 + core[0] * 8, 8)], mine.at[pl.ds(g * 8, 8)], sem_mine
            ).start()
            pltpu.make_async_copy(
                out_v.at[pl.ds(g * 16 + (1 - core[0]) * 8, 8)], theirs.at[pl.ds(g * 8, 8)], sem_theirs
            ).start()
    pltpu.make_async_copy(mine, mine, sem_mine).wait()
    pltpu.make_async_copy(theirs, theirs, sem_theirs).wait()


def rotate(core, slots, weights, arrived, left, right):
    half = jax.ShapeDtypeStruct((left.shape[0] // 2,) + left.shape[1:], jnp.bfloat16)
    anywhere = pl.BlockSpec(memory_space=pl.ANY)
    return pl.pallas_call(
        rotate_kernel,
        grid_spec=pltpu.PrefetchScalarGridSpec(
            num_scalar_prefetch=3,
            grid=(),
            in_specs=[anywhere] * 3,
            out_specs=[anywhere] * 2,
            scratch_shapes=[
                pltpu.VMEM(arrived.shape, jnp.bfloat16),
                pltpu.VMEM(left.shape, jnp.bfloat16),
                pltpu.VMEM(left.shape, jnp.bfloat16),
                pltpu.VMEM(left.shape, jnp.bfloat16),
                pltpu.SemaphoreType.DMA,
                pltpu.SemaphoreType.DMA((CHUNKS,)),
                pltpu.SemaphoreType.DMA((CHUNKS,)),
                pltpu.SemaphoreType.DMA,
                pltpu.SemaphoreType.DMA,
            ],
        ),
        out_shape=[half, half],
        name="rotate",
    )(core, slots, weights, arrived, left, right)


def panel_kernel(place, mine, other, *refs):
    pieces, rest = refs[:10], refs[10:]
    out, mine_v, other_v, vec_v, out_v, sem_rows, sem_vec, sem_out = rest
    copies = [
        pltpu.make_async_copy(mine, mine_v, sem_rows.at[0]),
        pltpu.make_async_copy(other, other_v, sem_rows.at[1]),
    ]
    half = vec_v.shape[2] // 2
    vec_copies = []
    for side in range(2):
        own, before, after, top, bottom = pieces[side * 5 : side * 5 + 5]
        targets = (
            (own, vec_v.at[side, 0]),
            (after, vec_v.at[side, 1]),
            (top, vec_v.at[side, 2, pl.ds(0, half)]),
            (bottom, vec_v.at[side, 2, pl.ds(half, half)]),
            (before, vec_v.at[side, 3]),
        )
        vec_copies.append(
            [pltpu.make_async_copy(a, b, sem_vec.at[side, n]) for n, (a, b) in enumerate(targets)]
        )
    for copy in copies + vec_copies[0] + vec_copies[1]:
        copy.start()
    for copy in copies:
        copy.wait()
    groups = mine_v.shape[0] // 8
    for side in range(2):
        for copy in vec_copies[side]:
            copy.wait()
        order = (mine_v, other_v) if side == 0 else (other_v, mine_v)

        def part(rel, carry):
            lhs = jnp.concatenate(
                [
                    jnp.concatenate([order[q][g * 8 + c] for c in range(8) for q in range(2)], axis=1)
                    for g in range(groups)
                ],
                axis=0,
            )
            rhs = vec_v[side, rel].reshape(-1, vec_v.shape[-1])
            out_v[side * 4 + rel] = (
                jnp.dot(lhs, rhs, preferred_element_type=jnp.float32)
                .astype(jnp.bfloat16)
                .reshape(out_v.shape[1:])
            )
            core = place[1] if side == 0 else 1 - place[1]
            target = lax.rem(place[0] + rel, 4) * 2 + core
            pltpu.make_async_copy(out_v.at[side * 4 + rel], out.at[:, target], sem_out).start()
            return carry

        lax.fori_loop(0, 4, part, 0)
    pltpu.make_async_copy(out_v, out_v, sem_out).wait()


def panel_product(place, mine, other, pieces):
    groups = mine.shape[0] // 8
    size = mine.shape[1]
    width = pieces[0].shape[-1]
    anywhere = pl.BlockSpec(memory_space=pl.ANY)
    return pl.pallas_call(
        panel_kernel,
        grid_spec=pltpu.PrefetchScalarGridSpec(
            num_scalar_prefetch=1,
            grid=(),
            in_specs=[anywhere] * 12,
            out_specs=anywhere,
            scratch_shapes=[
                pltpu.VMEM(mine.shape, jnp.bfloat16),
                pltpu.VMEM(mine.shape, jnp.bfloat16),
                pltpu.VMEM((2, 4) + pieces[0].shape, jnp.bfloat16),
                pltpu.VMEM((8, groups, size, width), jnp.bfloat16),
                pltpu.SemaphoreType.DMA((2,)),
                pltpu.SemaphoreType.DMA((2, 5)),
                pltpu.SemaphoreType.DMA,
            ],
        ),
        out_shape=jax.ShapeDtypeStruct((groups, 8, size, width), jnp.bfloat16),
        name="panel",
    )(place, mine, other, *pieces)


def shift(value, axis, step):
    count = lax.axis_size(axis)
    return lax.ppermute(value, axis, [(i, (i + step) % count) for i in range(count)])


def trial_pieces(trial):
    z = lax.axis_index("z")
    core = lax.axis_index("core")
    rows, wide = trial.shape
    width = wide // 8
    piece = lax.dynamic_slice_in_dim(trial, (z * 2 + core) * width, width, axis=1)
    piece = piece.reshape(2, 8, rows // 16, width)
    piece = jnp.where(core == 0, piece, piece[::-1])
    piece = jnp.transpose(piece, (1, 0, 2, 3))
    own = lax.all_to_all(piece, COL, split_axis=0, concat_axis=0, tiled=True)
    before = shift(own, "z", 1)
    after = shift(own, "z", -1)
    top = shift(before[:4], "z", 1)
    bottom = shift(after[4:], "z", -1)
    held = (own, before, after, top, bottom)
    return held + tuple(shift(value, "core", 1) for value in held)


def shards(coarse_kernel, interp_index, interp_weight, left_rot, right_rot, trial):
    dev_count = lax.axis_size(ALL)
    core = lax.axis_index("core").astype(jnp.int32)
    coarse_per = coarse_kernel.shape[0]
    pieces = trial_pieces(trial)
    ref_ids = interp_index.reshape(-1)
    catalog = jnp.arange(dev_count * coarse_per, dtype=jnp.int32)
    needed = (
        jnp.any(ref_ids[:, None] == catalog[None, :], axis=0)
        .astype(jnp.int32)
        .reshape(dev_count, coarse_per)
    )
    slot_rank = jnp.cumsum(needed, axis=1) - needed
    picker = needed[:, :, None] * (
        slot_rank[:, :, None] == jnp.arange(CAP, dtype=jnp.int32)[None, None, :]
    ).astype(jnp.int32)
    wanted = jnp.sum(picker * jnp.arange(coarse_per, dtype=jnp.int32)[None, :, None], axis=1)
    requested = lax.all_to_all(wanted, ALL, split_axis=0, concat_axis=0, tiled=True)
    served = serve(requested.reshape(-1), coarse_kernel).reshape(
        (dev_count, CAP) + coarse_kernel.shape[1:]
    )
    arrived = lax.all_to_all(served, ALL, split_axis=0, concat_axis=0, tiled=True)
    arrived = arrived.reshape((dev_count * CAP,) + coarse_kernel.shape[1:])
    slot_table = (jnp.arange(dev_count, dtype=jnp.int32)[:, None] * CAP + slot_rank).reshape(-1)
    ref_slots = jnp.take(slot_table, ref_ids, mode="clip")
    mine, theirs = rotate(
        core.reshape(1), ref_slots, interp_weight.reshape(-1), arrived, left_rot, right_rot
    )
    other = shift(theirs, "core", 1)
    place = jnp.stack([lax.axis_index("z").astype(jnp.int32), core])
    partial_product = panel_product(place, mine, other, pieces)
    groups, parts, size, width = partial_product.shape
    shares = lax.all_to_all(
        partial_product.reshape(groups * parts, size, width),
        SAME_CORE, split_axis=0, concat_axis=0, tiled=True,
    )
    shares = shares.reshape(groups, parts, size, width).astype(jnp.float32)
    return jnp.sum(shares, axis=1).reshape(groups * size, width)


def solution(mesh):
    cube = Mesh(mesh.devices.reshape(2, 4, 2, 4, 2), ALL)
    rows, cols = ALL[:3], ALL[3:]
    return jax.shard_map(
        shards,
        mesh=cube,
        in_specs=(
            P(ALL, None, None),
            P(ALL, None),
            P(ALL, None),
            P(ALL, None, None),
            P(ALL, None, None),
            P(cols, None),
        ),
        out_specs=P(rows, cols),
        check_vma=False,
    )
```

```python
import jax
import jax.numpy as jnp
from jax import lax
from jax.experimental import pallas as pl
from jax.experimental.pallas import tpu as pltpu
from jax.sharding import Mesh, PartitionSpec as P

CAP = 2
CHUNKS = 4
ROOM = 24 * 2**20
ALL = ("ylo", "z", "core", "x", "yhi")
COL = ("x", "yhi")
SAME_CORE = ("ylo", "z", "x", "yhi")


def serve_kernel(wanted, coarse, out, sem):
    def issue(i, carry):
        pltpu.make_async_copy(coarse.at[wanted[i]], out.at[i], sem).start()
        return carry

    lax.fori_loop(0, out.shape[0], issue, 0, unroll=8)
    pltpu.make_async_copy(out, out, sem).wait()


def serve(wanted, coarse_kernel):
    count = wanted.shape[0]
    return pl.pallas_call(
        serve_kernel,
        grid_spec=pltpu.PrefetchScalarGridSpec(
            num_scalar_prefetch=1,
            grid=(),
            in_specs=[pl.BlockSpec(memory_space=pltpu.VMEM)],
            out_specs=pl.BlockSpec(memory_space=pl.ANY),
            scratch_shapes=[pltpu.SemaphoreType.DMA],
        ),
        out_shape=pltpu.HBM((count,) + coarse_kernel.shape[1:], coarse_kernel.dtype),
        name="serve",
    )(wanted, coarse_kernel)


def near(value):
    return pltpu.with_memory_space_constraint(value, pltpu.VMEM)


def far(value):
    return pltpu.with_memory_space_constraint(value, pltpu.HBM)


def split(value):
    high = value.astype(jnp.bfloat16)
    low = (value - high.astype(jnp.float32)).astype(jnp.bfloat16)
    return high, low


def rotate_kernel(
    core, slots, weights, arrived, left, right, mine, theirs, left_v, right_v, sem_left, sem_right
):
    blocks = left.shape[0]
    span = blocks // CHUNKS
    copies = []
    for n in range(CHUNKS):
        part = pl.ds(n * span, span)
        pair = (
            pltpu.make_async_copy(left.at[part], left_v.at[part], sem_left.at[n]),
            pltpu.make_async_copy(right.at[part], right_v.at[part], sem_right.at[n]),
        )
        for copy in pair:
            copy.start()
        copies.append(pair)

    def block(f, out, place):
        r = f * 4
        merged = weights[r] * arrived[slots[r]].astype(jnp.float32)
        for j in range(1, 4):
            merged += weights[r + j] * arrived[slots[r + j]].astype(jnp.float32)
        lhs = left_v[f]
        turned = jnp.dot(
            jnp.concatenate([lhs, lhs], axis=1),
            jnp.concatenate(split(merged), axis=0),
            preferred_element_type=jnp.float32,
        )
        rhs = right_v[f]
        fine = lax.dot_general(
            jnp.concatenate(split(turned), axis=1),
            jnp.concatenate([rhs, rhs], axis=1),
            (((1,), (1,)), ((), ())),
            preferred_element_type=jnp.float32,
        )
        out[place] = fine.astype(jnp.bfloat16)

    for n in range(CHUNKS):
        for copy in copies[n]:
            copy.wait()

        def several(i, carry):
            group = n * (span // 16) + i
            for k in range(8):
                block(group * 16 + core[0] * 8 + k, mine, group * 8 + k)
                block(group * 16 + (1 - core[0]) * 8 + k, theirs, group * 8 + k)
            return carry

        lax.fori_loop(0, span // 16, several, 0)


def rotate(core, slots, weights, arrived, left, right):
    half = jax.ShapeDtypeStruct((left.shape[0] // 2,) + left.shape[1:], jnp.bfloat16)
    anywhere = pl.BlockSpec(memory_space=pl.ANY)
    local = pl.BlockSpec(memory_space=pltpu.VMEM)
    return pl.pallas_call(
        rotate_kernel,
        grid_spec=pltpu.PrefetchScalarGridSpec(
            num_scalar_prefetch=3,
            grid=(),
            in_specs=[local, anywhere, anywhere],
            out_specs=[local, local],
            scratch_shapes=[
                pltpu.VMEM(left.shape, jnp.bfloat16),
                pltpu.VMEM(left.shape, jnp.bfloat16),
                pltpu.SemaphoreType.DMA((CHUNKS,)),
                pltpu.SemaphoreType.DMA((CHUNKS,)),
            ],
        ),
        out_shape=[half, half],
        compiler_params=pltpu.CompilerParams(vmem_limit_bytes=ROOM),
        name="rotate",
    )(core, slots, weights, arrived, far(left), far(right))


def panel_kernel(place, mine, other, *refs):
    pieces, out, out_v, sem = refs[:14], refs[14], refs[15], refs[16]
    groups = mine.shape[0] // 8
    for side in range(2):
        held = pieces[side * 7 : side * 7 + 7]
        own, before, after, beyond = held[:1], held[1:3], held[3:5], held[5:]
        order = (mine, other) if side == 0 else (other, mine)
        core = place[1] if side == 0 else 1 - place[1]
        for rel, parts in enumerate((own, after, beyond, before)):
            lhs = jnp.concatenate(
                [
                    jnp.concatenate(
                        [
                            order[q][g * 8 + n]
                            for n in range(8)
                            for q in range(2)
                        ],
                        axis=1,
                    )
                    for g in range(groups)
                ],
                axis=0,
            )
            rhs = jnp.concatenate([p[...].reshape(-1, p.shape[-1]) for p in parts], axis=0)
            slot = side * 4 + rel
            out_v[slot] = (
                jnp.dot(lhs, rhs, preferred_element_type=jnp.float32)
                .astype(jnp.bfloat16)
                .reshape(out_v.shape[1:])
            )
            target = lax.rem(place[0] + rel, 4) * 2 + core
            pltpu.make_async_copy(out_v.at[slot], out.at[:, target], sem).start()
    pltpu.make_async_copy(out_v, out_v, sem).wait()


def panel_product(place, mine, other, pieces):
    groups = mine.shape[0] // 8
    size = mine.shape[1]
    width = pieces[0].shape[-1]
    local = pl.BlockSpec(memory_space=pltpu.VMEM)
    return pl.pallas_call(
        panel_kernel,
        grid_spec=pltpu.PrefetchScalarGridSpec(
            num_scalar_prefetch=1,
            grid=(),
            in_specs=[local] * (2 + len(pieces)),
            out_specs=pl.BlockSpec(memory_space=pl.ANY),
            scratch_shapes=[
                pltpu.VMEM((8, groups, size, width), jnp.bfloat16),
                pltpu.SemaphoreType.DMA,
            ],
        ),
        out_shape=pltpu.HBM((groups, 8, size, width), jnp.bfloat16),
        compiler_params=pltpu.CompilerParams(vmem_limit_bytes=ROOM),
        name="panel",
    )(place, mine, near(other), *map(near, pieces))


def shift(value, axis, step):
    count = lax.axis_size(axis)
    return lax.ppermute(value, axis, [(i, (i + step) % count) for i in range(count)])


def trial_pieces(trial):
    z = lax.axis_index("z")
    core = lax.axis_index("core")
    rows, wide = trial.shape
    width = wide // 8
    piece = lax.dynamic_slice_in_dim(trial, (z * 2 + core) * width, width, axis=1)
    piece = piece.reshape(2, 8, rows // 16, width)
    piece = jnp.where(core == 0, piece, piece[::-1])
    piece = jnp.transpose(piece, (1, 0, 2, 3))
    own = lax.all_to_all(piece, COL, split_axis=0, concat_axis=0, tiled=True)
    halves = own[:4], own[4:]
    before = [shift(half, "z", 1) for half in halves]
    after = [shift(half, "z", -1) for half in halves]
    top = shift(before[0], "z", 1)
    bottom = shift(after[1], "z", -1)
    early = [shift(value, "core", 1) for value in (own, *before, *after)]
    late = [shift(value, "core", 1) for value in (top, bottom)]
    return (own, *before, *after, top, bottom, *early, *late)


def shards(coarse_kernel, interp_index, interp_weight, left_rot, right_rot, trial):
    dev_count = lax.axis_size(ALL)
    core = lax.axis_index("core").astype(jnp.int32)
    coarse_per = coarse_kernel.shape[0]
    place = jnp.stack([lax.axis_index("z").astype(jnp.int32), core])
    pieces = trial_pieces(trial)
    ref_ids = interp_index.reshape(-1)
    catalog = jnp.arange(dev_count * coarse_per, dtype=jnp.int32)
    needed = (
        jnp.any(ref_ids[:, None] == catalog[None, :], axis=0)
        .astype(jnp.int32)
        .reshape(dev_count, coarse_per)
    )
    slot_rank = jnp.cumsum(needed, axis=1) - needed
    picker = needed[:, :, None] * (
        slot_rank[:, :, None] == jnp.arange(CAP, dtype=jnp.int32)[None, None, :]
    ).astype(jnp.int32)
    wanted = jnp.sum(picker * jnp.arange(coarse_per, dtype=jnp.int32)[None, :, None], axis=1)
    requested = lax.all_to_all(wanted, ALL, split_axis=0, concat_axis=0, tiled=True)
    served = serve(requested.reshape(-1), coarse_kernel).reshape(
        (dev_count, CAP) + coarse_kernel.shape[1:]
    )
    arrived = lax.all_to_all(served, ALL, split_axis=0, concat_axis=0, tiled=True)
    arrived = arrived.reshape((dev_count * CAP,) + coarse_kernel.shape[1:])
    slot_table = (jnp.arange(dev_count, dtype=jnp.int32)[:, None] * CAP + slot_rank).reshape(-1)
    ref_slots = jnp.take(slot_table, ref_ids, mode="clip")
    mine, theirs = rotate(
        core.reshape(1), ref_slots, interp_weight.reshape(-1), arrived, left_rot, right_rot
    )
    other = shift(theirs, "core", 1)
    partial_product = panel_product(place, mine, other, pieces)
    groups, parts, size, width = partial_product.shape
    shares = lax.all_to_all(
        partial_product.reshape(groups * parts, size, width),
        SAME_CORE, split_axis=0, concat_axis=0, tiled=True,
    )
    shares = shares.reshape(groups, parts, size, width).astype(jnp.float32)
    return jnp.sum(shares, axis=1).reshape(groups * size, width)


def solution(mesh):
    cube = Mesh(mesh.devices.reshape(2, 4, 2, 4, 2), ALL)
    rows, cols = ALL[:3], ALL[3:]
    return jax.shard_map(
        shards,
        mesh=cube,
        in_specs=(
            P(ALL, None, None),
            P(ALL, None),
            P(ALL, None),
            P(ALL, None, None),
            P(ALL, None, None),
            P(cols, None),
        ),
        out_specs=P(rows, cols),
        check_vma=False,
    )
```

```python
import jax
import jax.numpy as jnp
from jax import lax
from jax.experimental import pallas as pl
from jax.experimental.pallas import tpu as pltpu
from jax.sharding import Mesh, PartitionSpec as P

CAP = 2
ROOM = 24 * 2**20
ALL = ("ylo", "z", "core", "x", "yhi")
COL = ("x", "yhi")
SAME_CORE = ("ylo", "z", "x", "yhi")


def serve_kernel(wanted, coarse, out, sem):
    def issue(i, carry):
        pltpu.make_async_copy(coarse.at[wanted[i]], out.at[i], sem).start()
        return carry

    lax.fori_loop(0, out.shape[0], issue, 0, unroll=8)
    pltpu.make_async_copy(out, out, sem).wait()


def serve(wanted, coarse_kernel):
    count = wanted.shape[0]
    return pl.pallas_call(
        serve_kernel,
        grid_spec=pltpu.PrefetchScalarGridSpec(
            num_scalar_prefetch=1,
            grid=(),
            in_specs=[pl.BlockSpec(memory_space=pltpu.VMEM)],
            out_specs=pl.BlockSpec(memory_space=pl.ANY),
            scratch_shapes=[pltpu.SemaphoreType.DMA],
        ),
        out_shape=pltpu.HBM((count,) + coarse_kernel.shape[1:], coarse_kernel.dtype),
        name="serve",
    )(wanted, coarse_kernel)


def near(value):
    return pltpu.with_memory_space_constraint(value, pltpu.VMEM)


def far(value):
    return pltpu.with_memory_space_constraint(value, pltpu.HBM)


def split(value):
    high = value.astype(jnp.bfloat16)
    low = (value - high.astype(jnp.float32)).astype(jnp.bfloat16)
    return high, low


def fetch_rotate_kernel(
    core, slots, weights, arrived, left, right, out, held, left_v, right_v, sem_left, sem_right, sem
):
    copy = pltpu.make_async_copy(arrived, held, sem)
    copy.start()
    rotate_kernel(
        core, slots, weights, held, left, right, out, left_v, right_v, sem_left, sem_right, copy
    )


def rotate_kernel(
    core, slots, weights, arrived, left, right, out, left_v, right_v, sem_left, sem_right, first=None
):
    groups = out.shape[0] // 8
    copies = []
    for g in range(groups):
        held = pl.ds(g * 16 + core[0] * 8, 8)
        part = pl.ds(g * 8, 8)
        pair = (
            pltpu.make_async_copy(left.at[held], left_v.at[part], sem_left.at[g]),
            pltpu.make_async_copy(right.at[held], right_v.at[part], sem_right.at[g]),
        )
        for copy in pair:
            copy.start()
        copies.append(pair)
    if first is not None:
        first.wait()

    def block(f, place):
        r = f * 4
        merged = weights[r] * arrived[slots[r]].astype(jnp.float32)
        for j in range(1, 4):
            merged += weights[r + j] * arrived[slots[r + j]].astype(jnp.float32)
        lhs = left_v[place]
        turned = jnp.dot(
            jnp.concatenate([lhs, lhs], axis=1),
            jnp.concatenate(split(merged), axis=0),
            preferred_element_type=jnp.float32,
        )
        rhs = right_v[place]
        fine = lax.dot_general(
            jnp.concatenate(split(turned), axis=1),
            jnp.concatenate([rhs, rhs], axis=1),
            (((1,), (1,)), ((), ())),
            preferred_element_type=jnp.float32,
        )
        out[place] = fine.astype(jnp.bfloat16)

    for g in range(0, groups, 2):
        for copy in copies[g] + copies[g + 1]:
            copy.wait()
        for k in range(16):
            block((g + k // 8) * 16 + core[0] * 8 + k % 8, g * 8 + k)


def rotate(core, slots, weights, arrived, left, right, fetch):
    half = (left.shape[0] // 2,) + left.shape[1:]
    anywhere = pl.BlockSpec(memory_space=pltpu.HBM)
    local = pl.BlockSpec(memory_space=pltpu.VMEM)
    out = jax.ShapeDtypeStruct(half, jnp.bfloat16)
    sems = pltpu.SemaphoreType.DMA((half[0] // 8,))
    return pl.pallas_call(
        fetch_rotate_kernel if fetch else rotate_kernel,
        grid_spec=pltpu.PrefetchScalarGridSpec(
            num_scalar_prefetch=3,
            grid=(),
            in_specs=[anywhere if fetch else local, anywhere, anywhere],
            out_specs=[local, local] if fetch else local,
            scratch_shapes=[
                pltpu.VMEM(half, jnp.bfloat16),
                pltpu.VMEM(half, jnp.bfloat16),
                sems,
                sems,
            ]
            + [pltpu.SemaphoreType.DMA] * fetch,
        ),
        out_shape=[out, pltpu.VMEM(arrived.shape, arrived.dtype)] if fetch else out,
        compiler_params=pltpu.CompilerParams(vmem_limit_bytes=ROOM),
        name="rotate",
    )(core, slots, weights, far(arrived) if fetch else arrived, far(left), far(right))


def panel_kernel(place, mine, other, *refs):
    pieces, out, out_v, sem = refs[:14], refs[14], refs[15], refs[16]
    groups = mine.shape[0] // 8
    for side in range(2):
        held = pieces[side * 7 : side * 7 + 7]
        own, before, after, beyond = held[:1], held[1:3], held[3:5], held[5:]
        order = (mine, other) if side == 0 else (other, mine)
        core = place[1] if side == 0 else 1 - place[1]
        for rel, parts in enumerate((own, after, beyond, before)):
            lhs = jnp.concatenate(
                [
                    jnp.concatenate(
                        [
                            order[q][g * 8 + n]
                            for n in range(8)
                            for q in range(2)
                        ],
                        axis=1,
                    )
                    for g in range(groups)
                ],
                axis=0,
            )
            rhs = jnp.concatenate([p[...].reshape(-1, p.shape[-1]) for p in parts], axis=0)
            slot = side * 4 + rel
            out_v[slot] = (
                jnp.dot(lhs, rhs, preferred_element_type=jnp.float32)
                .astype(jnp.bfloat16)
                .reshape(out_v.shape[1:])
            )
            target = lax.rem(place[0] + rel, 4) * 2 + core
            pltpu.make_async_copy(out_v.at[slot], out.at[:, target], sem).start()
    pltpu.make_async_copy(out_v, out_v, sem).wait()


def panel_product(place, mine, other, pieces):
    groups = mine.shape[0] // 8
    size = mine.shape[1]
    width = pieces[0].shape[-1]
    local = pl.BlockSpec(memory_space=pltpu.VMEM)
    return pl.pallas_call(
        panel_kernel,
        grid_spec=pltpu.PrefetchScalarGridSpec(
            num_scalar_prefetch=1,
            grid=(),
            in_specs=[local] * (2 + len(pieces)),
            out_specs=pl.BlockSpec(memory_space=pl.ANY),
            scratch_shapes=[
                pltpu.VMEM((8, groups, size, width), jnp.bfloat16),
                pltpu.SemaphoreType.DMA,
            ],
        ),
        out_shape=pltpu.HBM((groups, 8, size, width), jnp.bfloat16),
        compiler_params=pltpu.CompilerParams(vmem_limit_bytes=ROOM),
        name="panel",
    )(place, mine, near(other), *map(near, pieces))


def shift(value, axis, step):
    count = lax.axis_size(axis)
    return lax.ppermute(value, axis, [(i, (i + step) % count) for i in range(count)])


def trial_pieces(trial):
    z = lax.axis_index("z")
    core = lax.axis_index("core")
    rows, wide = trial.shape
    width = wide // 8
    piece = lax.dynamic_slice_in_dim(trial, (z * 2 + core) * width, width, axis=1)
    piece = piece.reshape(2, 8, rows // 16, width)
    piece = jnp.where(core == 0, piece, piece[::-1])
    piece = jnp.transpose(piece, (1, 0, 2, 3))
    own = lax.all_to_all(piece, COL, split_axis=0, concat_axis=0, tiled=True)
    halves = own[:4], own[4:]
    before = [shift(half, "z", 1) for half in halves]
    after = [shift(half, "z", -1) for half in halves]
    top = shift(before[0], "z", 1)
    bottom = shift(after[1], "z", -1)
    early = [shift(value, "core", 1) for value in (own, *before, *after)]
    late = [shift(value, "core", 1) for value in (top, bottom)]
    return (own, *before, *after, top, bottom, *early, *late)


def shards(coarse_kernel, interp_index, interp_weight, left_rot, right_rot, trial):
    dev_count = lax.axis_size(ALL)
    core = lax.axis_index("core").astype(jnp.int32)
    coarse_per = coarse_kernel.shape[0]
    place = jnp.stack([lax.axis_index("z").astype(jnp.int32), core])
    pieces = trial_pieces(trial)
    ref_ids = interp_index.reshape(-1)
    catalog = jnp.arange(dev_count * coarse_per, dtype=jnp.int32)
    needed = (
        jnp.any(ref_ids[:, None] == catalog[None, :], axis=0)
        .astype(jnp.int32)
        .reshape(dev_count, coarse_per)
    )
    slot_rank = jnp.cumsum(needed, axis=1) - needed
    picker = needed[:, :, None] * (
        slot_rank[:, :, None] == jnp.arange(CAP, dtype=jnp.int32)[None, None, :]
    ).astype(jnp.int32)
    wanted = jnp.sum(picker * jnp.arange(coarse_per, dtype=jnp.int32)[None, :, None], axis=1)
    requested = lax.all_to_all(wanted, ALL, split_axis=0, concat_axis=0, tiled=True)
    served = serve(requested.reshape(-1), coarse_kernel)
    served = served.reshape((dev_count, CAP) + coarse_kernel.shape[1:])
    arrived = lax.all_to_all(served, ALL, split_axis=0, concat_axis=0, tiled=True)
    arrived = arrived.reshape((dev_count * CAP,) + coarse_kernel.shape[1:])
    slot_table = (jnp.arange(dev_count, dtype=jnp.int32)[:, None] * CAP + slot_rank).reshape(-1)
    ref_slots = jnp.take(slot_table, ref_ids, mode="clip")
    weights = interp_weight.reshape(-1)
    rots = left_rot, right_rot
    theirs, held = rotate((1 - core).reshape(1), ref_slots, weights, arrived, *rots, True)
    mine = rotate(core.reshape(1), ref_slots, weights, held, *rots, False)
    other = shift(theirs, "core", 1)
    partial_product = panel_product(place, mine, other, pieces)
    groups, parts, size, width = partial_product.shape
    shares = lax.all_to_all(
        partial_product.reshape(groups * parts, size, width),
        SAME_CORE, split_axis=0, concat_axis=0, tiled=True,
    )
    shares = shares.reshape(groups, parts, size, width).astype(jnp.float32)
    return jnp.sum(shares, axis=1).reshape(groups * size, width)


def solution(mesh):
    cube = Mesh(mesh.devices.reshape(2, 4, 2, 4, 2), ALL)
    rows, cols = ALL[:3], ALL[3:]
    return jax.shard_map(
        shards,
        mesh=cube,
        in_specs=(
            P(ALL, None, None),
            P(ALL, None),
            P(ALL, None),
            P(ALL, None, None),
            P(ALL, None, None),
            P(cols, None),
        ),
        out_specs=P(rows, cols),
        check_vma=False,
    )
```

```python
import jax
import jax.numpy as jnp
from jax import lax
from jax.experimental import pallas as pl
from jax.experimental.pallas import tpu as pltpu
from jax.sharding import Mesh, PartitionSpec as P

CAP = 2
ROOM = 24 * 2**20
ALL = ("ylo", "z", "core", "x", "yhi")
COL = ("x", "yhi")
SAME_CORE = ("ylo", "z", "x", "yhi")


def serve_kernel(wanted, coarse, out, sem):
    def issue(i, carry):
        pltpu.make_async_copy(coarse.at[wanted[i]], out.at[i], sem).start()
        return carry

    lax.fori_loop(0, out.shape[0], issue, 0, unroll=8)
    pltpu.make_async_copy(out, out, sem).wait()


def serve(wanted, coarse_kernel):
    count = wanted.shape[0]
    return pl.pallas_call(
        serve_kernel,
        grid_spec=pltpu.PrefetchScalarGridSpec(
            num_scalar_prefetch=1,
            grid=(),
            in_specs=[pl.BlockSpec(memory_space=pltpu.VMEM)],
            out_specs=pl.BlockSpec(memory_space=pl.ANY),
            scratch_shapes=[pltpu.SemaphoreType.DMA],
        ),
        out_shape=pltpu.HBM((count,) + coarse_kernel.shape[1:], coarse_kernel.dtype),
        name="serve",
    )(wanted, coarse_kernel)


def near(value):
    return pltpu.with_memory_space_constraint(value, pltpu.VMEM)


def far(value):
    return pltpu.with_memory_space_constraint(value, pltpu.HBM)


def split(value):
    high = value.astype(jnp.bfloat16)
    low = (value - high.astype(jnp.float32)).astype(jnp.bfloat16)
    return high, low


def fetch_rotate_kernel(
    core, slots, weights, arrived, left, right, out, held, left_v, right_v, sem_left, sem_right, sem
):
    copy = pltpu.make_async_copy(arrived, held, sem)
    copy.start()
    rotate_kernel(
        core, slots, weights, held, left, right, out, left_v, right_v, sem_left, sem_right, copy
    )


def rotate_kernel(
    core, slots, weights, arrived, left, right, out, left_v, right_v, sem_left, sem_right, first=None
):
    groups = out.shape[0] // 8
    copies = []
    for g in range(groups):
        held = pl.ds(g * 16 + core[0] * 8, 8)
        part = pl.ds(g * 8, 8)
        pair = (
            pltpu.make_async_copy(left.at[held], left_v.at[part], sem_left.at[g]),
            pltpu.make_async_copy(right.at[held], right_v.at[part], sem_right.at[g]),
        )
        for copy in pair:
            copy.start()
        copies.append(pair)
    if first is not None:
        first.wait()

    def block(f, place):
        r = f * 4
        merged = weights[r] * arrived[slots[r]].astype(jnp.float32)
        for j in range(1, 4):
            merged += weights[r + j] * arrived[slots[r + j]].astype(jnp.float32)
        lhs = left_v[place]
        turned = jnp.dot(
            jnp.concatenate([lhs, lhs], axis=1),
            jnp.concatenate(split(merged), axis=0),
            preferred_element_type=jnp.float32,
        )
        rhs = right_v[place]
        fine = lax.dot_general(
            jnp.concatenate(split(turned), axis=1),
            jnp.concatenate([rhs, rhs], axis=1),
            (((1,), (1,)), ((), ())),
            preferred_element_type=jnp.float32,
        )
        out[place] = fine.astype(jnp.bfloat16)

    for g in range(0, groups, 2):
        for copy in copies[g] + copies[g + 1]:
            copy.wait()
        for k in range(16):
            block((g + k // 8) * 16 + core[0] * 8 + k % 8, g * 8 + k)


def rotate(core, slots, weights, arrived, left, right, fetch):
    half = (left.shape[0] // 2,) + left.shape[1:]
    anywhere = pl.BlockSpec(memory_space=pltpu.HBM)
    local = pl.BlockSpec(memory_space=pltpu.VMEM)
    out = jax.ShapeDtypeStruct(half, jnp.bfloat16)
    sems = pltpu.SemaphoreType.DMA((half[0] // 8,))
    return pl.pallas_call(
        fetch_rotate_kernel if fetch else rotate_kernel,
        grid_spec=pltpu.PrefetchScalarGridSpec(
            num_scalar_prefetch=3,
            grid=(),
            in_specs=[anywhere if fetch else local, anywhere, anywhere],
            out_specs=[local, local] if fetch else local,
            scratch_shapes=[
                pltpu.VMEM(half, jnp.bfloat16),
                pltpu.VMEM(half, jnp.bfloat16),
                sems,
                sems,
            ]
            + [pltpu.SemaphoreType.DMA] * fetch,
        ),
        out_shape=[out, pltpu.VMEM(arrived.shape, arrived.dtype)] if fetch else out,
        compiler_params=pltpu.CompilerParams(vmem_limit_bytes=ROOM),
        name="rotate",
    )(core, slots, weights, far(arrived) if fetch else arrived, far(left), far(right))


def panel_kernel(place, mine, other, *refs):
    pieces, out, out_v, sem = refs[:16], refs[16], refs[17], refs[18]
    groups = mine.shape[0] // 8
    for side in range(2):
        held = pieces[side * 8 : side * 8 + 8]
        own, before, after, beyond = held[:2], held[2:4], held[4:6], held[6:]
        order = (mine, other) if side == 0 else (other, mine)
        core = place[1] if side == 0 else 1 - place[1]
        for rel, parts in enumerate((own, after, beyond, before)):
            lhs = jnp.concatenate(
                [
                    jnp.concatenate(
                        [
                            order[q][g * 8 + n]
                            for n in range(8)
                            for q in range(2)
                        ],
                        axis=1,
                    )
                    for g in range(groups)
                ],
                axis=0,
            )
            near_half, far_half = [p[...].reshape(-1, p.shape[-1]) for p in parts]
            first = place[2] == 0
            rhs = jnp.concatenate(
                [
                    jnp.where(first, near_half, far_half),
                    jnp.where(first, far_half, near_half),
                ],
                axis=1,
            )
            slot = side * 4 + rel
            out_v[slot] = (
                jnp.dot(lhs, rhs, preferred_element_type=jnp.float32)
                .astype(jnp.bfloat16)
                .reshape(out_v.shape[1:])
            )
            target = lax.rem(place[0] + rel, 4) * 2 + core
            pltpu.make_async_copy(out_v.at[slot], out.at[:, target], sem).start()
    pltpu.make_async_copy(out_v, out_v, sem).wait()


def panel_product(place, mine, other, pieces):
    groups = mine.shape[0] // 8
    size = mine.shape[1]
    width = pieces[0].shape[-1] * 2
    local = pl.BlockSpec(memory_space=pltpu.VMEM)
    return pl.pallas_call(
        panel_kernel,
        grid_spec=pltpu.PrefetchScalarGridSpec(
            num_scalar_prefetch=1,
            grid=(),
            in_specs=[local] * (2 + len(pieces)),
            out_specs=pl.BlockSpec(memory_space=pl.ANY),
            scratch_shapes=[
                pltpu.VMEM((8, groups, size, width), jnp.bfloat16),
                pltpu.SemaphoreType.DMA,
            ],
        ),
        out_shape=pltpu.HBM((groups, 8, size, width), jnp.bfloat16),
        compiler_params=pltpu.CompilerParams(vmem_limit_bytes=ROOM),
        name="panel",
    )(place, mine, near(other), *map(near, pieces))


def shift(value, axis, step):
    count = lax.axis_size(axis)
    return lax.ppermute(value, axis, [(i, (i + step) % count) for i in range(count)])


def trial_pieces(trial):
    ylo = lax.axis_index("ylo")
    z = lax.axis_index("z")
    core = lax.axis_index("core")
    rows, wide = trial.shape
    width = wide // 16
    piece = lax.dynamic_slice_in_dim(trial, ((z * 2 + core) * 2 + ylo) * width, width, axis=1)
    piece = piece.reshape(2, 8, rows // 16, width)
    piece = jnp.where(core == 0, piece, piece[::-1])
    piece = jnp.transpose(piece, (1, 0, 2, 3))
    own = lax.all_to_all(piece, COL, split_axis=0, concat_axis=0, tiled=True)
    twin = shift(own, "ylo", 1)
    before, after = [shift(own, "z", 1)], [shift(own, "z", -1)]
    before.append(shift(twin, "z", 1))
    after.append(shift(twin, "z", -1))
    top = shift(before[0], "z", 1)
    bottom = shift(top, "ylo", 1)
    early = [shift(value, "core", 1) for value in (own, twin, *before, *after)]
    late = [shift(value, "core", 1) for value in (top, bottom)]
    return (own, twin, *before, *after, top, bottom, *early, *late)


def shards(coarse_kernel, interp_index, interp_weight, left_rot, right_rot, trial):
    dev_count = lax.axis_size(ALL)
    core = lax.axis_index("core").astype(jnp.int32)
    coarse_per = coarse_kernel.shape[0]
    place = jnp.stack([lax.axis_index(axis).astype(jnp.int32) for axis in ("z", "core", "ylo")])
    pieces = trial_pieces(trial)
    ref_ids = interp_index.reshape(-1)
    catalog = jnp.arange(dev_count * coarse_per, dtype=jnp.int32)
    needed = (
        jnp.any(ref_ids[:, None] == catalog[None, :], axis=0)
        .astype(jnp.int32)
        .reshape(dev_count, coarse_per)
    )
    slot_rank = jnp.cumsum(needed, axis=1) - needed
    picker = needed[:, :, None] * (
        slot_rank[:, :, None] == jnp.arange(CAP, dtype=jnp.int32)[None, None, :]
    ).astype(jnp.int32)
    wanted = jnp.sum(picker * jnp.arange(coarse_per, dtype=jnp.int32)[None, :, None], axis=1)
    requested = lax.all_to_all(wanted, ALL, split_axis=0, concat_axis=0, tiled=True)
    served = serve(requested.reshape(-1), coarse_kernel)
    served = served.reshape((dev_count, CAP) + coarse_kernel.shape[1:])
    arrived = lax.all_to_all(served, ALL, split_axis=0, concat_axis=0, tiled=True)
    arrived = arrived.reshape((dev_count * CAP,) + coarse_kernel.shape[1:])
    slot_table = (jnp.arange(dev_count, dtype=jnp.int32)[:, None] * CAP + slot_rank).reshape(-1)
    ref_slots = jnp.take(slot_table, ref_ids, mode="clip")
    weights = interp_weight.reshape(-1)
    rots = left_rot, right_rot
    theirs, held = rotate((1 - core).reshape(1), ref_slots, weights, arrived, *rots, True)
    mine = rotate(core.reshape(1), ref_slots, weights, held, *rots, False)
    other = shift(theirs, "core", 1)
    partial_product = panel_product(place, mine, other, pieces)
    groups, parts, size, width = partial_product.shape
    shares = lax.all_to_all(
        partial_product.reshape(groups * parts, size, width),
        SAME_CORE, split_axis=0, concat_axis=0, tiled=True,
    )
    shares = shares.reshape(groups, parts, size, width).astype(jnp.float32)
    return jnp.sum(shares, axis=1).reshape(groups * size, width)


def solution(mesh):
    cube = Mesh(mesh.devices.reshape(2, 4, 2, 4, 2), ALL)
    rows, cols = ALL[:3], ALL[3:]
    return jax.shard_map(
        shards,
        mesh=cube,
        in_specs=(
            P(ALL, None, None),
            P(ALL, None),
            P(ALL, None),
            P(ALL, None, None),
            P(ALL, None, None),
            P(cols, None),
        ),
        out_specs=P(rows, cols),
        check_vma=False,
    )
```
